32 devices in a mesh: dp: 2 (over y), row: 4 (over z), col: 4 (over x, core).
Axes of the slice: x: 2, y: 2, z: 4, core: 2. Of those that a mesh axis runs over, the one named last changes fastest.
Arguments:
- latents: bfloat16 [16, 1024, 1408], P(('dp', 'row'), None, 'col'), may hold values from -6 to 6
- skip_latents: bfloat16 [16, 1024, 1408], P(('dp', 'row'), None, 'col'), may hold values from -6 to 6
- text_states: bfloat16 [16, 333, 1024], P(('dp', 'row'), None, 'col'), may hold values from -6 to 6
- condition: bfloat16 [16, 1408], P(('dp', 'row')), may hold values from -6 to 6
- positions: int32 [16, 2, 1024], P(('dp', 'row')), may hold values from 0 to 63, as said below
- cotangent: bfloat16 [16, 1024, 1408], P(('dp', 'row'), None, 'col'), may hold values from -6 to 6
- w_skip: bfloat16 [2, 1408, 1408], P(None, ('dp', 'row'), 'col'), may hold values from -0.109375 to 0.109375
- g_skip: float32 [2, 1408], P(None, 'col'), may hold values from 0.1 to 1.9
- g_norm1: float32 [1408], P('col'), may hold values from 0.1 to 1.9
- w_mod: bfloat16 [1408, 1408], P(('dp', 'row'), 'col'), may hold values from -0.15625 to 0.15625
- w_qkv: bfloat16 [3, 1408, 1408], P(None, ('dp', 'row'), 'col'), may hold values from -0.15625 to 0.15625
- g_query: float32 [88], replicated, may hold values from 1 to 1.8
- g_key: float32 [88], replicated, may hold values from 1 to 1.8
- w_out: bfloat16 [1408, 1408], P('col', ('dp', 'row')), may hold values from -2.5 to 2.5
- g_norm3: float32 [1408], P('col'), may hold values from 0.1 to 1.9
- w_cross_q: bfloat16 [1408, 1408], P(('dp', 'row'), 'col'), may hold values from -0.15625 to 0.15625
- w_cross_kv: bfloat16 [2, 1024, 1408], P(None, ('dp', 'row'), 'col'), may hold values from -0.1875 to 0.1875
- g_cross_q: float32 [88], replicated, may hold values from 1 to 1.8
- g_cross_k: float32 [88], replicated, may hold values from 1 to 1.8
- w_cross_out: bfloat16 [1408, 1408], P('col', ('dp', 'row')), may hold values from -1.75 to 1.75
- g_norm2: float32 [1408], P('col'), may hold values from 0.1 to 1.9
- w_fc1: bfloat16 [1408, 6144], P(('dp', 'row'), 'col'), may hold values from -0.15625 to 0.15625
- w_fc2: bfloat16 [6144, 1408], P('col', ('dp', 'row')), may hold values from -0.078125 to 0.078125
Outputs:
- output: bfloat16 [16, 1024, 1408], P(('dp', 'row'), None, 'col')
- grad_latents: float32 [16, 1024, 1408], P(('dp', 'row'), None, 'col')
- grad_skip: float32 [16, 1024, 1408], P(('dp', 'row'), None, 'col')
- grad_text: float32 [16, 333, 1024], P(('dp', 'row'), None, 'col')
- grad_w_skip: float32 [2, 1408, 1408], P(None, ('dp', 'row'), 'col')
- grad_g_skip: float32 [2, 1408], P(None, 'col')
- grad_g_norm1: float32 [1408], P('col')
- grad_w_mod: float32 [1408, 1408], P(('dp', 'row'), 'col')
- grad_w_qkv: float32 [3, 1408, 1408], P(None, ('dp', 'row'), 'col')
- grad_g_query: float32 [88], replicated
- grad_g_key: float32 [88], replicated
- grad_w_out: float32 [1408, 1408], P('col', ('dp', 'row'))
- grad_g_norm3: float32 [1408], P('col')
- grad_w_cross_q: float32 [1408, 1408], P(('dp', 'row'), 'col')
- grad_w_cross_kv: float32 [2, 1024, 1408], P(None, ('dp', 'row'), 'col')
- grad_g_cross_q: float32 [88], replicated
- grad_g_cross_k: float32 [88], replicated
- grad_w_cross_out: float32 [1408, 1408], P('col', ('dp', 'row'))
- grad_g_norm2: float32 [1408], P('col')
- grad_w_fc1: float32 [1408, 6144], P(('dp', 'row'), 'col')
- grad_w_fc2: float32 [6144, 1408], P('col', ('dp', 'row'))
The draws below stay inside these ranges and needn't reach their ends.
Inputs may be any that keep to these rules, and one draw needn't show every extreme that they name: `positions`: token t of a sequence sits at grid row t // w and grid column t % w, where w is that sequence's grid width, one of 16, 32 and 64; every draw holds sequences of width 16 and of width 64.
All inputs are finite; a program needn't handle non-finite values.
Results may differ from the reference program's by a relative error of at most 0.03.
Values may be sent and summed in bfloat16 or wider, within the bound.
No kernel may reach another device: no remote copies, remote signals or barrier semaphores. Data moves between devices by JAX's collectives and lax.ppermute only.
A program may use at most 248 MiB of HBM per device.

```python
import jax
import jax.numpy as jnp
from jax import lax

D = 1408
TEXT_D = 1024
HEAD_DIM = 88
FF = 6144
LEN = 1024
TEXT = 333
SEQS = 16


def draw_positions(key, part):
    width_pick = jax.random.randint(key, (SEQS,), 0, 3)
    width_pick = width_pick.at[0].set(2).at[1].set(0)
    grid_width = jnp.where(width_pick == 0, 16, jnp.where(width_pick == 1, 32, 64)).astype(jnp.int32)
    token_index = jnp.arange(LEN, dtype=jnp.int32)
    grid_rows = token_index[None, :] // grid_width[:, None]
    grid_cols = token_index[None, :] % grid_width[:, None]
    return jnp.stack([grid_rows, grid_cols], 1).astype(jnp.int32)


def block_levels(key, extent, shards, smallest, high):
    level = 1.0
    for dim, shards_of in shards:
        heights = jax.random.uniform(jax.random.fold_in(jax.random.fold_in(key, 6), dim), (shards_of,), jnp.float32, smallest / len(shards), high / len(shards))
        level = level * jnp.repeat(jnp.exp(heights), extent[dim] // shards_of).reshape((-1,) + (1,) * (len(extent) - 1 - dim))
    return level


def gaussian(key, shape, scale, most, split=(), held_as=jnp.bfloat16):
    level = block_levels(key, shape, split, -0.22, 0.18) if split else 1.0
    entries = jax.random.normal(key, shape, jnp.float32) * scale * level
    return jnp.minimum(jnp.maximum(entries, -most), most).astype(held_as)


def setup_inputs(seed: int = 0) -> dict:
    streams_of = jax.random.split(jax.random.key(seed), 24)
    return {
        "latents": gaussian(streams_of[0], (SEQS, LEN, D), 1.0, 6.0, ((0, 8), (2, 4))),
        "skip_latents": gaussian(streams_of[1], (SEQS, LEN, D), 1.0, 6.0, ((0, 8), (2, 4))),
        "text_states": gaussian(streams_of[2], (SEQS, TEXT, TEXT_D), 1.0, 6.0, ((0, 8), (2, 4))),
        "condition": gaussian(streams_of[3], (SEQS, D), 1.0, 6.0, ((0, 8),)),
        "positions": draw_positions(jax.random.fold_in(streams_of[23], 71), 0),
        "cotangent": gaussian(streams_of[5], (SEQS, LEN, D), 1.0, 6.0, ((0, 8), (2, 4))),
        "w_skip": gaussian(streams_of[6], (2, D, D), (2 * D) ** -0.5, 0.109375, ((1, 8), (2, 4))),
        "g_skip": jnp.clip(1.0 + 0.18 * jax.random.normal(streams_of[7], (2, D), jnp.float32), 0.1, 1.9),
        "g_norm1": jnp.clip(1.0 + 0.18 * jax.random.normal(streams_of[8], (D,), jnp.float32), 0.1, 1.9),
        "w_mod": gaussian(streams_of[9], (D, D), D ** -0.5, 0.15625, ((0, 8), (1, 4))),
        "w_qkv": gaussian(streams_of[10], (3, D, D), D ** -0.5, 0.15625, ((1, 8), (2, 4))),
        "g_query": jnp.clip(jax.random.uniform(streams_of[11], (HEAD_DIM,), jnp.float32, 1.0, 1.8), 1.0, 1.8),
        "g_key": jnp.clip(jax.random.uniform(streams_of[12], (HEAD_DIM,), jnp.float32, 1.0, 1.8), 1.0, 1.8),
        "w_out": gaussian(streams_of[13], (D, D), (max(D // 256, 1)) ** -0.5, 2.5, ((0, 4), (1, 8))),
        "g_norm3": jnp.clip(1.0 + 0.18 * jax.random.normal(streams_of[14], (D,), jnp.float32), 0.1, 1.9),
        "w_cross_q": gaussian(streams_of[15], (D, D), D ** -0.5, 0.15625, ((0, 8), (1, 4))),
        "w_cross_kv": gaussian(streams_of[16], (2, TEXT_D, D), TEXT_D ** -0.5, 0.1875, ((1, 8), (2, 4))),
        "g_cross_q": jnp.clip(jax.random.uniform(streams_of[17], (HEAD_DIM,), jnp.float32, 1.0, 1.8), 1.0, 1.8),
        "g_cross_k": jnp.clip(jax.random.uniform(streams_of[18], (HEAD_DIM,), jnp.float32, 1.0, 1.8), 1.0, 1.8),
        "w_cross_out": gaussian(streams_of[19], (D, D), (max(D // 128, 1)) ** -0.5, 1.75, ((0, 4), (1, 8))),
        "g_norm2": jnp.clip(1.0 + 0.18 * jax.random.normal(streams_of[20], (D,), jnp.float32), 0.1, 1.9),
        "w_fc1": gaussian(streams_of[21], (D, FF), D ** -0.5, 0.15625, ((0, 8), (1, 4))),
        "w_fc2": gaussian(streams_of[22], (FF, D), FF ** -0.5, 0.078125, ((0, 4), (1, 8))),
    }


epsilon = 1e-06
rope_base = 10000.0
highest = lax.Precision.HIGHEST

@jax.custom_vjp
def low(v):
    return lax.optimization_barrier(v.astype(jnp.bfloat16)).astype(jnp.float32)

@jax.custom_vjp
def low_back(v):
    return v

def low_keep(v):
    return (low(v), None)

def low_pass(kept, grad):
    return (grad,)

def back_keep(v):
    return (v, None)

def back_low(kept, grad):
    return (low(grad),)
low.defvjp(low_keep, low_pass)
low_back.defvjp(back_keep, back_low)

def layer_norm(values, gain):
    average = lax.optimization_barrier(jnp.mean(values, -1, keepdims=True))
    centered = values - average
    variance = lax.optimization_barrier(jnp.mean(centered * centered, -1, keepdims=True))
    return centered * lax.rsqrt(variance + epsilon) * gain

def head_split(values):
    return values.reshape(values.shape[:-1] + (values.shape[-1] // HEAD_DIM, HEAD_DIM))

def head_norm(values, gain):
    return layer_norm(head_split(values), gain).reshape(values.shape)

def rotary_tables(positions):
    quarter = HEAD_DIM // 4
    frequency = rope_base ** (-(jnp.arange(quarter, dtype=jnp.float32) / quarter))
    rows_angle = positions[..., 0, :].astype(jnp.float32)[..., None] * frequency
    cols_angle = positions[..., 1, :].astype(jnp.float32)[..., None] * frequency
    angles = jnp.concatenate([rows_angle, cols_angle, rows_angle, cols_angle], -1)
    return (jnp.cos(angles), jnp.sin(angles))

def rotate(values, cosine, sine_table):
    shaped = head_split(values)
    middle = HEAD_DIM // 2
    turned = jnp.concatenate([-shaped[..., middle:], shaped[..., :middle]], -1)
    result = shaped * cosine[..., :, None, :] + turned * sine_table[..., :, None, :]
    return result.reshape(values.shape)

def linear(values, weight):
    return jnp.einsum('...d,de->...e', values, weight, precision=highest)

def attend(parts):
    query_rows, key_rows, value_rows = parts
    query_heads = head_split(query_rows)
    key_heads = head_split(key_rows)
    value_heads = head_split(value_rows)
    scores = jnp.einsum('qhd,khd->hqk', query_heads, key_heads, precision=highest) * HEAD_DIM ** (-0.5)
    softmax_weights = jax.nn.softmax(low_back(scores), axis=-1)
    mixed = jnp.einsum('hqk,khd->qhd', low(softmax_weights), value_heads, precision=highest)
    return mixed.reshape(query_rows.shape)

def block(params, image_in, skip_in, text_in, cond_in, cosine, sine_table):
    w_skip, g_skip, g_norm1, w_mod, w_qkv, g_query, g_key, w_out, g_norm3, w_cross_q, w_cross_kv, g_cross_q, g_cross_k, w_cross_out, g_norm2, w_fc1, w_fc2 = params
    model_width = image_in.shape[-1]
    joined = jnp.concatenate([image_in, skip_in], -1)
    normed = low(layer_norm(joined, g_skip.reshape(-1)))
    stream0 = low_back(linear(normed[..., :model_width], w_skip[0]) + linear(normed[..., model_width:], w_skip[1]))
    ada_shift = jnp.einsum('gd,de->ge', low(jax.nn.silu(cond_in)), w_mod, precision=highest)
    ada_in = low(layer_norm(stream0, g_norm1) + ada_shift[:, None, :])
    query_raw = low_back(linear(ada_in, w_qkv[0]))
    key_raw = low_back(linear(ada_in, w_qkv[1]))
    value_raw = low_back(linear(ada_in, w_qkv[2]))
    query_hat = low(rotate(head_norm(query_raw, g_query), cosine, sine_table))
    key_hat = low(rotate(head_norm(key_raw, g_key), cosine, sine_table))
    attended = lax.map(jax.checkpoint(attend), (query_hat, key_hat, low(value_raw)))
    attended = low(low_back(attended))
    stream1 = stream0 + low_back(linear(attended, w_out))
    cross_in = low(layer_norm(stream1, g_norm3))
    cross_query = low_back(linear(cross_in, w_cross_q))
    cross_key = low_back(linear(text_in, w_cross_kv[0]))
    cross_value = low_back(linear(text_in, w_cross_kv[1]))
    crossed = lax.map(jax.checkpoint(attend), (low(rotate(head_norm(cross_query, g_cross_q), cosine, sine_table)), low(head_norm(cross_key, g_cross_k)), low(cross_value)))
    crossed = low(low_back(crossed))
    stream2 = stream1 + low_back(linear(crossed, w_cross_out))
    mlp_in = low(layer_norm(stream2, g_norm2))
    hidden = low(jax.nn.gelu(low_back(linear(mlp_in, w_fc1)), approximate=True))
    return stream2 + low_back(linear(hidden, w_fc2))

def reference(latents, skip_latents, text_states, condition, positions, cotangent, w_skip, g_skip, g_norm1, w_mod, w_qkv, g_query, g_key, w_out, g_norm3, w_cross_q, w_cross_kv, g_cross_q, g_cross_k, w_cross_out, g_norm2, w_fc1, w_fc2):
    params = tuple((weight.astype(jnp.float32) for weight in (w_skip, g_skip, g_norm1, w_mod, w_qkv, g_query, g_key, w_out, g_norm3, w_cross_q, w_cross_kv, g_cross_q, g_cross_k, w_cross_out, g_norm2, w_fc1, w_fc2)))
    group_size = 4
    group_count = latents.shape[0] // group_size

    def regroup(values):
        return values.reshape((group_count, group_size) + values.shape[1:])

    def group_step(totals, batch_item):
        image_group, skip_group, text_group, cond_group, place_group, grad_group = batch_item
        cosine, sine_table = rotary_tables(place_group)
        cond_float = cond_group.astype(jnp.float32)

        def forward(weights, image_in, skip_in, text_in):
            return block(weights, image_in, skip_in, text_in, cond_float, cosine, sine_table)
        result, pullback = jax.vjp(forward, params, image_group.astype(jnp.float32), skip_group.astype(jnp.float32), text_group.astype(jnp.float32))
        gradients = pullback(grad_group.astype(jnp.float32))
        totals = jax.tree.map(lambda earlier, addend: earlier + addend, totals, gradients[0])
        return (totals, (result.astype(jnp.bfloat16), gradients[1], gradients[2], gradients[3]))
    zero_grads = jax.tree.map(jnp.zeros_like, params)
    totals, stacked = lax.scan(group_step, zero_grads, tuple((regroup(values) for values in (latents, skip_latents, text_states, condition, positions, cotangent))))
    output, grad_latents, grad_skip, grad_text = (values.reshape((-1,) + values.shape[2:]) for values in stacked)
    grad_w_skip, grad_g_skip, grad_g_norm1, grad_w_mod, grad_w_qkv, grad_g_query, grad_g_key, grad_w_out, grad_g_norm3, grad_w_cross_q, grad_w_cross_kv, grad_g_cross_q, grad_g_cross_k, grad_w_cross_out, grad_g_norm2, grad_w_fc1, grad_w_fc2 = totals
    return (output, grad_latents, grad_skip, grad_text, grad_w_skip, grad_g_skip, grad_g_norm1, grad_w_mod, grad_w_qkv, grad_g_query, grad_g_key, grad_w_out, grad_g_norm3, grad_w_cross_q, grad_w_cross_kv, grad_g_cross_q, grad_g_cross_k, grad_w_cross_out, grad_g_norm2, grad_w_fc1, grad_w_fc2)
```

```python
import jax
import jax.numpy as jnp
from jax import lax
from jax.sharding import PartitionSpec as P

HEAD = 88
EPS = 1e-06
BASE = 10000.0
WIDE = ("dp", "row")
NEAR, FAR = 1, 2
ORDER = (0, FAR, NEAR, NEAR | FAR)
F32, BF16 = jnp.float32, jnp.bfloat16


def dot(spec, left, right):
    return jnp.einsum(spec, left, right, preferred_element_type=F32)


def swap(values, bit):
    return lax.ppermute(values, "col", [(i, i ^ bit) for i in range(4)])


def spread(values):
    far = swap(values, FAR)
    return jnp.concatenate([values, far, swap(values, NEAR), swap(far, NEAR)], 0)


def settle(partial):
    low = partial.astype(BF16)
    size = low.shape[0] // 4
    pair = low[: 2 * size].astype(F32) + swap(low[2 * size :], NEAR).astype(F32)
    return pair[:size] + swap(pair[size:].astype(BF16), FAR).astype(F32)


def total(values):
    return (values + swap(values, FAR)) + (swap(values, NEAR) + swap(values, NEAR | FAR))


def to_relative(values, me):
    blocks = values.reshape((4, values.shape[0] // 4) + values.shape[1:])
    return jnp.concatenate(
        [lax.dynamic_index_in_dim(blocks, me ^ m, 0, keepdims=False) for m in ORDER], 0
    )


def to_canonical(values, me):
    blocks = values.reshape((4, values.shape[0] // 4) + values.shape[1:])
    place = jnp.array(ORDER, jnp.int32)
    return jnp.concatenate(
        [lax.dynamic_index_in_dim(blocks, place[me ^ b], 0, keepdims=False) for b in range(4)], 0
    )


def norm(members, width):
    first = sum(jnp.sum(m, 0) for m in members)
    second = sum(jnp.sum(m * m, 0) for m in members)
    sums = total(jnp.stack([first, second]))
    average = sums[0] / width
    scale = lax.rsqrt(sums[1] / width - average * average + EPS)
    return tuple((m - average) * scale for m in members), scale


def norm_back(grads, normals, scale, width):
    first = sum(jnp.sum(g, 0) for g in grads)
    second = sum(jnp.sum(g * n, 0) for g, n in zip(grads, normals))
    sums = total(jnp.stack([first, second])) / width
    return tuple((g - sums[0] - n * sums[1]) * scale for g, n in zip(grads, normals))


def heads(values):
    return values.reshape((values.shape[0] // HEAD, HEAD) + values.shape[1:])


def head_norm(values):
    split = heads(values)
    centered = split - jnp.mean(split, 1, keepdims=True)
    scale = lax.rsqrt(jnp.mean(centered * centered, 1, keepdims=True) + EPS)
    return centered * scale, scale


def head_norm_back(grad, gain, normal, scale):
    gain_grad = jnp.sum(grad * normal, (0, 2))
    g = grad * gain[:, None]
    mean_one = jnp.mean(g, 1, keepdims=True)
    mean_two = jnp.mean(g * normal, 1, keepdims=True)
    value = (g - mean_one - normal * mean_two) * scale
    return value.reshape((-1,) + value.shape[2:]), gain_grad


def tables(positions):
    quarter = HEAD // 4
    frequency = BASE ** (-(jnp.arange(quarter, dtype=F32) / quarter))
    place = positions.astype(F32)
    angles = jnp.concatenate([frequency[:, None] * place[0], frequency[:, None] * place[1]], 0)
    return jnp.cos(angles), jnp.sin(angles)


def rope(values, cosine, sine):
    one, two = values[:, : HEAD // 2], values[:, HEAD // 2 :]
    return jnp.concatenate([one * cosine - two * sine, two * cosine + one * sine], 1)


def rope_back(values, cosine, sine):
    one, two = values[:, : HEAD // 2], values[:, HEAD // 2 :]
    return jnp.concatenate([one * cosine + two * sine, two * cosine - one * sine], 1)


SCALE = HEAD**-0.5


def attend(query, key, value):
    scores = dot("hdq,hdk->hqk", query, key) * SCALE
    top = jnp.max(scores, -1, keepdims=True)
    grown = jnp.exp(scores - top)
    sums = jnp.sum(grown, -1, keepdims=True)
    weights = (grown / sums).astype(BF16)
    mixed = dot("hqk,hdk->hdq", weights, value)
    return mixed.reshape((-1, mixed.shape[2])).astype(BF16), top + jnp.log(sums)


def attend_back(query, key, value, logs, grad):
    weights = jnp.exp(dot("hdq,hdk->hqk", query, key) * SCALE - logs)
    grad_value = dot("hqk,hdq->hdk", weights.astype(BF16), grad)
    grad_weights = dot("hdq,hdk->hqk", grad, value)
    mean = jnp.sum(weights * grad_weights, -1, keepdims=True)
    grad_scores = (weights * (grad_weights - mean)).astype(BF16)
    grad_query = dot("hqk,hdk->hdq", grad_scores, key) * SCALE
    grad_key = dot("hqk,hdq->hdk", grad_scores, query) * SCALE
    return grad_query, grad_key, grad_value


def gelu(u):
    return jax.nn.gelu(u, approximate=True)


def flat(values):
    return values.reshape((-1,) + values.shape[2:])


def shards(
    latents,
    skip_latents,
    text_states,
    condition,
    positions,
    cotangent,
    w_skip,
    g_skip,
    g_norm1,
    w_mod,
    w_qkv,
    g_query,
    g_key,
    w_out,
    g_norm3,
    w_cross_q,
    w_cross_kv,
    g_cross_q,
    g_cross_k,
    w_cross_out,
    g_norm2,
    w_fc1,
    w_fc2,
):
    me = lax.axis_index("col")
    count = latents.shape[0]
    each = range(count)
    width = 4 * latents.shape[2]
    part = latents.shape[2]

    def gather(shard):
        return to_relative(lax.all_gather(shard, WIDE, axis=0, tiled=True), me)

    def scatter(grad):
        return lax.psum_scatter(
            to_canonical(grad.astype(BF16), me), WIDE, scatter_dimension=0, tiled=True
        ).astype(F32)

    full_skip = gather(jnp.concatenate([w_skip[0], w_skip[1]], 1))
    full_qkv = gather(jnp.concatenate([w_qkv[0], w_qkv[1], w_qkv[2]], 1))
    full_out = gather(w_out.T)
    full_cross_q = gather(w_cross_q)
    full_cross_kv = gather(jnp.concatenate([w_cross_kv[0], w_cross_kv[1]], 1))
    full_cross_out = gather(w_cross_out.T)
    full_fc1 = gather(w_fc1)
    full_fc2 = gather(w_fc2.T)

    cond_low = jax.nn.silu(condition.astype(F32)).astype(BF16)
    cond_all = lax.all_gather(cond_low, WIDE, axis=0, tiled=True)
    wide_index = lax.axis_index(WIDE)
    cond_mine = lax.dynamic_slice_in_dim(
        cond_all, wide_index * w_mod.shape[0], w_mod.shape[0], axis=1
    )
    shift = lax.psum_scatter(
        dot("sd,de->se", cond_mine, w_mod), WIDE, scatter_dimension=0, tiled=True
    )

    col = lambda gain: gain[:, None]
    image = [latents[i].T.astype(F32) for i in each]
    skip = [skip_latents[i].T.astype(F32) for i in each]
    text_full = [spread(text_states[i].T) for i in each]
    cot = [cotangent[i].T for i in each]
    turn = [tables(positions[i]) for i in each]

    normal_in, scale_in = zip(*[norm((image[i], skip[i]), 2 * width) for i in each])
    image_full = [spread((normal_in[i][0] * col(g_skip[0])).astype(BF16)) for i in each]
    skip_full = [spread((normal_in[i][1] * col(g_skip[1])).astype(BF16)) for i in each]
    stream0 = [
        dot("de,dt->et", full_skip[:, :part], image_full[i])
        + dot("de,dt->et", full_skip[:, part:], skip_full[i])
        for i in each
    ]
    normal_one, scale_one = zip(*[norm((stream0[i],), width) for i in each])
    ada_full = [
        spread((normal_one[i][0] * col(g_norm1) + col(shift[i])).astype(BF16)) for i in each
    ]
    projected = [dot("de,dt->et", full_qkv, ada_full[i]) for i in each]
    query_norm, key_norm, query_hat, key_hat, value_hat = [], [], [], [], []
    attended, logs = [], []
    for i in each:
        qn = head_norm(projected[i][:part])
        kn = head_norm(projected[i][part : 2 * part])
        query_norm.append(qn)
        key_norm.append(kn)
        query_hat.append(rope(qn[0] * col(g_query), *turn[i]).astype(BF16))
        key_hat.append(rope(kn[0] * col(g_key), *turn[i]).astype(BF16))
        value_hat.append(heads(projected[i][2 * part :].astype(BF16)))
        mixed, log_sums = attend(query_hat[i], key_hat[i], value_hat[i])
        attended.append(mixed)
        logs.append(log_sums)
    stream1 = [stream0[i] + settle(dot("ec,ct->et", full_out, attended[i])) for i in each]
    normal_three, scale_three = zip(*[norm((stream1[i],), width) for i in each])
    cross_full = [spread((normal_three[i][0] * col(g_norm3)).astype(BF16)) for i in each]
    cq_norm, ck_norm, cq_hat, ck_hat, cv_hat, crossed, cross_logs = [], [], [], [], [], [], []
    for i in each:
        qn = head_norm(dot("de,dt->et", full_cross_q, cross_full[i]))
        pair = dot("de,dt->et", full_cross_kv, text_full[i])
        kn = head_norm(pair[:part])
        cq_norm.append(qn)
        ck_norm.append(kn)
        cq_hat.append(rope(qn[0] * col(g_cross_q), *turn[i]).astype(BF16))
        ck_hat.append((kn[0] * col(g_cross_k)).astype(BF16))
        cv_hat.append(heads(pair[part:].astype(BF16)))
        mixed, log_sums = attend(cq_hat[i], ck_hat[i], cv_hat[i])
        crossed.append(mixed)
        cross_logs.append(log_sums)
    stream2 = [stream1[i] + settle(dot("ec,ct->et", full_cross_out, crossed[i])) for i in each]
    normal_two, scale_two = zip(*[norm((stream2[i],), width) for i in each])
    mlp_full = [spread((normal_two[i][0] * col(g_norm2)).astype(BF16)) for i in each]
    pre = [dot("de,dt->et", full_fc1, mlp_full[i]) for i in each]
    hidden, pulls = zip(*[jax.vjp(gelu, pre[i]) for i in each])
    hidden = [h.astype(BF16) for h in hidden]
    output = [
        (stream2[i] + settle(dot("ec,ct->et", full_fc2, hidden[i]))).astype(BF16) for i in each
    ]

    cot_full = [spread(cot[i]) for i in each]
    grad_pre = [
        pulls[i](dot("ec,et->ct", full_fc2, cot_full[i]))[0].astype(BF16) for i in each
    ]
    grad_fc2 = scatter(sum(dot("et,ct->ec", cot_full[i], hidden[i]) for i in each)).T
    grad_fc1 = scatter(sum(dot("dt,et->de", mlp_full[i], grad_pre[i]) for i in each))
    grad_mlp = [settle(dot("de,et->dt", full_fc1, grad_pre[i])) for i in each]
    gain_two = sum(jnp.sum(grad_mlp[i] * normal_two[i][0], 1) for i in each)
    grad_stream2 = [
        cot[i].astype(F32)
        + norm_back((grad_mlp[i] * col(g_norm2),), normal_two[i], scale_two[i], width)[0]
        for i in each
    ]
    gs2_full = [spread(grad_stream2[i].astype(BF16)) for i in each]
    grad_crossed = [
        heads(dot("ec,et->ct", full_cross_out, gs2_full[i]).astype(BF16)) for i in each
    ]
    grad_cross_out = scatter(sum(dot("et,ct->ec", gs2_full[i], crossed[i]) for i in each)).T
    grad_cq, grad_pair, gain_cq, gain_ck = [], [], [], []
    for i in each:
        gq, gk, gv = attend_back(cq_hat[i], ck_hat[i], cv_hat[i], cross_logs[i], grad_crossed[i])
        gq, gain_q = head_norm_back(rope_back(gq, *turn[i]), g_cross_q, *cq_norm[i])
        gk, gain_k = head_norm_back(gk, g_cross_k, *ck_norm[i])
        grad_cq.append(gq.astype(BF16))
        grad_pair.append(jnp.concatenate([gk, flat(gv)], 0).astype(BF16))
        gain_cq.append(gain_q)
        gain_ck.append(gain_k)
    grad_cross_q = scatter(sum(dot("dt,et->de", cross_full[i], grad_cq[i]) for i in each))
    grad_cross_kv = scatter(sum(dot("dt,et->de", text_full[i], grad_pair[i]) for i in each))
    grad_cross_in = [settle(dot("de,et->dt", full_cross_q, grad_cq[i])) for i in each]
    grad_text = [settle(dot("de,et->dt", full_cross_kv, grad_pair[i])) for i in each]
    gain_three = sum(jnp.sum(grad_cross_in[i] * normal_three[i][0], 1) for i in each)
    grad_stream1 = [
        grad_stream2[i]
        + norm_back((grad_cross_in[i] * col(g_norm3),), normal_three[i], scale_three[i], width)[0]
        for i in each
    ]
    gs1_full = [spread(grad_stream1[i].astype(BF16)) for i in each]
    grad_attended = [heads(dot("ec,et->ct", full_out, gs1_full[i]).astype(BF16)) for i in each]
    grad_out = scatter(sum(dot("et,ct->ec", gs1_full[i], attended[i]) for i in each)).T
    grad_qkv, gain_q_all, gain_k_all = [], [], []
    for i in each:
        gq, gk, gv = attend_back(query_hat[i], key_hat[i], value_hat[i], logs[i], grad_attended[i])
        gq, gain_q = head_norm_back(rope_back(gq, *turn[i]), g_query, *query_norm[i])
        gk, gain_k = head_norm_back(rope_back(gk, *turn[i]), g_key, *key_norm[i])
        grad_qkv.append(jnp.concatenate([gq, gk, flat(gv)], 0).astype(BF16))
        gain_q_all.append(gain_q)
        gain_k_all.append(gain_k)
    grad_qkv_w = scatter(sum(dot("dt,et->de", ada_full[i], grad_qkv[i]) for i in each))
    grad_ada = [settle(dot("de,et->dt", full_qkv, grad_qkv[i])) for i in each]
    grad_shift = jnp.stack([jnp.sum(grad_ada[i], 1) for i in each])
    grad_shift_all = lax.all_gather(grad_shift, WIDE, axis=0, tiled=True)
    grad_mod = jnp.einsum(
        "sd,se->de", cond_mine.astype(F32), grad_shift_all, precision=lax.Precision.HIGHEST
    )
    gain_one = sum(jnp.sum(grad_ada[i] * normal_one[i][0], 1) for i in each)
    grad_stream0 = [
        (
            grad_stream1[i]
            + norm_back((grad_ada[i] * col(g_norm1),), normal_one[i], scale_one[i], width)[0]
        ).astype(BF16)
        for i in each
    ]
    grad_skip_w = scatter(
        jnp.concatenate(
            [
                sum(dot("dt,et->de", image_full[i], grad_stream0[i]) for i in each),
                sum(dot("dt,et->de", skip_full[i], grad_stream0[i]) for i in each),
            ],
            1,
        )
    )
    back_image = [settle(dot("de,et->dt", full_skip[:, :part], grad_stream0[i])) for i in each]
    back_skip = [settle(dot("de,et->dt", full_skip[:, part:], grad_stream0[i])) for i in each]
    gain_image = sum(jnp.sum(back_image[i] * normal_in[i][0], 1) for i in each)
    gain_skip = sum(jnp.sum(back_skip[i] * normal_in[i][1], 1) for i in each)
    grad_in = [
        norm_back(
            (back_image[i] * col(g_skip[0]), back_skip[i] * col(g_skip[1])),
            normal_in[i],
            scale_in[i],
            2 * width,
        )
        for i in each
    ]
    head_sums = lax.psum(
        jnp.stack([sum(gain_q_all), sum(gain_k_all), sum(gain_cq), sum(gain_ck)]),
        ("dp", "row", "col"),
    )
    gain_sums = lax.psum(
        jnp.stack([gain_image, gain_skip, gain_one, gain_three, gain_two]), WIDE
    )
    unstack = lambda grad, n: jnp.stack(jnp.split(grad, n, 1))
    back = lambda rows: jnp.stack([r.T for r in rows])
    return (
        back(output),
        back([g[0] for g in grad_in]),
        back([g[1] for g in grad_in]),
        back(grad_text),
        unstack(grad_skip_w, 2),
        gain_sums[:2],
        gain_sums[2],
        grad_mod,
        unstack(grad_qkv_w, 3),
        head_sums[0],
        head_sums[1],
        grad_out,
        gain_sums[3],
        grad_cross_q,
        unstack(grad_cross_kv, 2),
        head_sums[2],
        head_sums[3],
        grad_cross_out,
        gain_sums[4],
        grad_fc1,
        grad_fc2,
    )


def solution(mesh):
    wide = ("dp", "row")
    tokens, rows, stacked, columns = (
        P(wide, None, "col"),
        P(wide, "col"),
        P(None, wide, "col"),
        P("col", wide),
    )
    gain = P("col")
    return jax.shard_map(
        shards,
        mesh=mesh,
        in_specs=(
            tokens,
            tokens,
            tokens,
            P(wide, None),
            P(wide, None, None),
            tokens,
            stacked,
            P(None, "col"),
            gain,
            rows,
            stacked,
            P(),
            P(),
            columns,
            gain,
            rows,
            stacked,
            P(),
            P(),
            columns,
            gain,
            rows,
            columns,
        ),
        out_specs=(
            tokens,
            tokens,
            tokens,
            tokens,
            stacked,
            P(None, "col"),
            gain,
            rows,
            stacked,
            P(),
            P(),
            columns,
            gain,
            rows,
            stacked,
            P(),
            P(),
            columns,
            gain,
            rows,
            columns,
        ),
        check_vma=False,
    )
```

```python
import functools

import jax
import jax.numpy as jnp
from jax import lax
from jax.experimental import pallas as pl
from jax.experimental.pallas import tpu as pltpu
from jax.sharding import PartitionSpec as P

HEAD = 88
HALF = HEAD // 2
EPS = 1e-06
BASE = 10000.0
SCALE = HEAD**-0.5
WIDE = ("dp", "row")
NEAR, FAR = 1, 2
ORDER = (0, FAR, NEAR, NEAR | FAR)
F32, BF16 = jnp.float32, jnp.bfloat16


def dot(spec, left, right):
    return jnp.einsum(spec, left, right, preferred_element_type=F32)


def swap(values, bit):
    return lax.ppermute(values, "col", [(i, i ^ bit) for i in range(4)])


def spread(values):
    far = swap(values, FAR)
    return [values, far, swap(values, NEAR), swap(far, NEAR)]


def settle(partial):
    low = partial.astype(BF16)
    size = low.shape[0] // 4
    pair = low[: 2 * size].astype(F32) + swap(low[2 * size :], NEAR).astype(F32)
    return pair[:size] + swap(pair[size:].astype(BF16), FAR).astype(F32)


def total(values):
    return (values + swap(values, FAR)) + (swap(values, NEAR) + swap(values, NEAR | FAR))


def wide_bits():
    bit = 1
    while bit < lax.axis_size("row") * lax.axis_size("dp"):
        yield bit
        bit *= 2


def wide_swap(values, bit):
    rows = lax.axis_size("row")
    axis, step = ("row", bit) if bit < rows else ("dp", bit // rows)
    return lax.ppermute(values, axis, [(i, i ^ step) for i in range(lax.axis_size(axis))])


def wide_gather(values):
    for bit in wide_bits():
        values = jnp.concatenate([values, wide_swap(values, bit)], 0)
    return values


def wide_scatter(values, kind):
    for bit in reversed(list(wide_bits())):
        half = values.shape[0] // 2
        moved = wide_swap(values[half:].astype(kind), bit)
        values = values[:half].astype(F32) + moved.astype(F32)
    return values


def wide_sum(values):
    for bit in wide_bits():
        values = values + wide_swap(values, bit)
    return values


def take_blocks(blocks, order):
    rows, columns = blocks.shape[1:]

    def kernel(order_ref, in_ref, out_ref):
        out_ref[...] = in_ref[...]

    count = order.shape[0]
    out = pl.pallas_call(
        kernel,
        out_shape=jax.ShapeDtypeStruct((count, rows, columns), blocks.dtype),
        grid_spec=pltpu.PrefetchScalarGridSpec(
            num_scalar_prefetch=1,
            grid=(count,),
            in_specs=[pl.BlockSpec((None, rows, columns), lambda i, o: (o[i], 0, 0))],
            out_specs=pl.BlockSpec((None, rows, columns), lambda i, o: (i, 0, 0)),
        ),
        name="take_blocks",
    )(order, blocks)
    return out.reshape(count * rows, columns)


def dot_nt(left, right):
    return lax.dot_general(left, right, (((1,), (1,)), ((), ())), preferred_element_type=F32)


def dot_tn(left, right):
    return lax.dot_general(left, right, (((0,), (0,)), ((), ())), preferred_element_type=F32)


def dot_nn(left, right):
    return lax.dot_general(left, right, (((1,), (0,)), ((), ())), preferred_element_type=F32)


def weight_grad(lefts, rights, order, turned):
    depth, tokens = lefts[0].shape
    columns = rights[0].shape[0]
    blocks = 4
    rows = depth // blocks
    n = len(lefts)

    def kernel(order_ref, turned_ref, *refs):
        out_ref = refs[-1]
        value = sum(dot_nt(refs[i][...], refs[n + i][...]) for i in range(n)).astype(BF16)
        half = rows // 2
        first = pl.multiple_of(turned_ref[0] * half, half)
        second = pl.multiple_of((1 - turned_ref[0]) * half, half)
        out_ref[pl.ds(first, half), :] = value[:half]
        out_ref[pl.ds(second, half), :] = value[half:]

    return pl.pallas_call(
        kernel,
        out_shape=jax.ShapeDtypeStruct((depth, columns), BF16),
        grid_spec=pltpu.PrefetchScalarGridSpec(
            num_scalar_prefetch=2,
            grid=(blocks,),
            in_specs=[pl.BlockSpec((rows, tokens), lambda i, o, t: (i, 0))] * n
            + [pl.BlockSpec((columns, r.shape[1]), lambda i, o, t: (0, 0)) for r in rights],
            out_specs=pl.BlockSpec((rows, columns), lambda i, o, t: (o[i], 0)),
        ),
        cost_estimate=pl.CostEstimate(
            flops=2 * n * depth * tokens * columns,
            transcendentals=0,
            bytes_accessed=2 * (n * (depth + columns) * tokens + depth * columns),
        ),
        name="weight_grad",
    )(order, turned, *lefts, *rights)


def normalize(values):
    centered = values - jnp.mean(values, 0, keepdims=True)
    scale = lax.rsqrt(jnp.mean(centered * centered, 0, keepdims=True) + EPS)
    return centered * scale, scale


def rope(values, cosine, sine):
    one, two = values[:HALF], values[HALF:]
    return jnp.concatenate([one * cosine - two * sine, two * cosine + one * sine], 0)


def rope_back(values, cosine, sine):
    one, two = values[:HALF], values[HALF:]
    return jnp.concatenate([one * cosine + two * sine, two * cosine - one * sine], 0)


def normalize_back(grad, gain, normal, scale):
    gain_grad = jnp.sum(grad * normal, 1, keepdims=True)
    g = grad * gain
    value = g - jnp.mean(g, 0, keepdims=True) - normal * jnp.mean(g * normal, 0, keepdims=True)
    return value * scale, gain_grad


CHUNK = 256
LOG2E = 1.4426950408889634


def attend(query, keys, values, gains, turn, key_turn, valid):
    heads = query[0].shape[0] if query[0].shape[0] == 4 else query[0].shape[0] // 3
    tokens, length = query[0].shape[2], keys[0].shape[2]

    def kernel(q_ref, k_ref, v_ref, gq_ref, gk_ref, c_ref, s_ref, o_ref, l_ref, qh_ref, kh_ref, vh_ref):
        cosine, sine = c_ref[...], s_ref[...]
        qh_ref[...] = rope(normalize(q_ref[...])[0] * gq_ref[...], cosine, sine).astype(BF16)
        key = normalize(k_ref[...])[0] * gk_ref[...]
        if key_turn:
            key = rope(key, cosine, sine)
        kh_ref[...] = key.astype(BF16)
        vh_ref[...] = v_ref[...].astype(BF16)
        for c in range(tokens // CHUNK):
            place = pl.ds(c * CHUNK, CHUNK)
            scores = dot_tn(kh_ref[...], qh_ref[:, place])
            if valid < length:
                row = lax.broadcasted_iota(jnp.int32, scores.shape, 0)
                scores = jnp.where(row < valid, scores, -1e30)
            top = jnp.max(scores, 0, keepdims=True)
            grown = jnp.exp2((scores - top) * (SCALE * LOG2E))
            sums = jnp.sum(grown, 0, keepdims=True)
            mixed = dot_nn(vh_ref[...], grown.astype(BF16))
            o_ref[:, place] = (mixed / sums).astype(BF16)
            l_ref[:, place] = top * SCALE + jnp.log(sums)

    def one(first, size):
        return pl.BlockSpec((None, HEAD, size), lambda h: (h + first, 0, 0))

    whole = lambda a: pl.BlockSpec(a.shape, lambda h: (0,) * a.ndim)
    extra = (gains[0][:, None], gains[1][:, None]) + turn
    mixed, logs = pl.pallas_call(
        kernel,
        out_shape=(
            jax.ShapeDtypeStruct((heads, HEAD, tokens), BF16),
            jax.ShapeDtypeStruct((heads, 1, tokens), F32),
        ),
        grid=(heads,),
        in_specs=[one(query[1], tokens), one(keys[1], length), one(values[1], length)]
        + [whole(a) for a in extra],
        out_specs=(
            pl.BlockSpec((None, HEAD, tokens), lambda h: (h, 0, 0)),
            pl.BlockSpec((None, 1, tokens), lambda h: (h, 0, 0)),
        ),
        scratch_shapes=[
            pltpu.VMEM((HEAD, tokens), BF16),
            pltpu.VMEM((HEAD, length), BF16),
            pltpu.VMEM((HEAD, length), BF16),
        ],
        cost_estimate=pl.CostEstimate(
            flops=4 * heads * HEAD * tokens * length,
            transcendentals=heads * tokens * length,
            bytes_accessed=heads * HEAD * (6 * tokens + 8 * length),
        ),
        name="attend",
    )(query[0], keys[0], values[0], *extra)
    return mixed.reshape(heads * HEAD, tokens), logs


def attend_back(query, keys, values, gains, turn, key_turn, valid, logs, grad):
    heads = logs.shape[0]
    tokens, length = query[0].shape[2], keys[0].shape[2]
    grad = grad.reshape(heads, HEAD, tokens)

    def kernel(
        q_ref, k_ref, v_ref, gq_ref, gk_ref, c_ref, s_ref, l_ref, g_ref,
        dq_ref, dkv_ref, dgq_ref, dgk_ref,
        qh_ref, kh_ref, vh_ref, tq_ref, tk_ref, tv_ref,
    ):
        cosine, sine = c_ref[...], s_ref[...]
        q_normal, q_scale = normalize(q_ref[...])
        k_normal, k_scale = normalize(k_ref[...])
        qh_ref[...] = rope(q_normal * gq_ref[...], cosine, sine).astype(BF16)
        key = k_normal * gk_ref[...]
        if key_turn:
            key = rope(key, cosine, sine)
        kh_ref[...] = key.astype(BF16)
        vh_ref[...] = v_ref[...].astype(BF16)
        for c in range(tokens // CHUNK):
            place = pl.ds(c * CHUNK, CHUNK)
            part, grad_part = qh_ref[:, place], g_ref[:, place]
            scores = dot_tn(kh_ref[...], part)
            weights = jnp.exp2((scores * SCALE - l_ref[:, place]) * LOG2E)
            if valid < length:
                row = lax.broadcasted_iota(jnp.int32, weights.shape, 0)
                weights = jnp.where(row < valid, weights, 0.0)
            grad_weights = dot_tn(vh_ref[...], grad_part)
            product = weights * grad_weights
            mean = jnp.sum(product, 0, keepdims=True)
            grad_scores = (product - weights * mean).astype(BF16)
            add_value = dot_nt(grad_part, weights.astype(BF16))
            add_key = dot_nt(part, grad_scores)
            tq_ref[:, place] = dot_nn(kh_ref[...], grad_scores)
            if c == 0:
                tv_ref[...], tk_ref[...] = add_value, add_key
            else:
                tv_ref[...] += add_value
                tk_ref[...] += add_key
        grad_q = rope_back(tq_ref[...] * SCALE, cosine, sine)
        grad_k = tk_ref[...] * SCALE
        if key_turn:
            grad_k = rope_back(grad_k, cosine, sine)
        q_out, gain_q = normalize_back(grad_q, gq_ref[...], q_normal, q_scale)
        k_out, gain_k = normalize_back(grad_k, gk_ref[...], k_normal, k_scale)
        dq_ref[...] = q_out.astype(BF16)
        dkv_ref[0] = k_out.astype(BF16)
        dkv_ref[1] = tv_ref[...].astype(BF16)
        dgq_ref[...] = gain_q
        dgk_ref[...] = gain_k

    def one(first, size):
        return pl.BlockSpec((None, HEAD, size), lambda h: (h + first, 0, 0))

    whole = lambda a: pl.BlockSpec(a.shape, lambda h: (0,) * a.ndim)
    extra = (gains[0][:, None], gains[1][:, None]) + turn
    dq, dkv, gain_q, gain_k = pl.pallas_call(
        kernel,
        out_shape=(
            jax.ShapeDtypeStruct((heads, HEAD, tokens), BF16),
            jax.ShapeDtypeStruct((2, heads, HEAD, length), BF16),
            jax.ShapeDtypeStruct((heads, HEAD, 1), F32),
            jax.ShapeDtypeStruct((heads, HEAD, 1), F32),
        ),
        grid=(heads,),
        in_specs=[one(query[1], tokens), one(keys[1], length), one(values[1], length)]
        + [whole(a) for a in extra]
        + [pl.BlockSpec((None, 1, tokens), lambda h: (h, 0, 0)), one(0, tokens)],
        out_specs=(
            pl.BlockSpec((None, HEAD, tokens), lambda h: (h, 0, 0)),
            pl.BlockSpec((2, None, HEAD, length), lambda h: (0, h, 0, 0)),
            pl.BlockSpec((None, HEAD, 1), lambda h: (h, 0, 0)),
            pl.BlockSpec((None, HEAD, 1), lambda h: (h, 0, 0)),
        ),
        scratch_shapes=[
            pltpu.VMEM((HEAD, tokens), BF16),
            pltpu.VMEM((HEAD, length), BF16),
            pltpu.VMEM((HEAD, length), BF16),
            pltpu.VMEM((HEAD, tokens), F32),
            pltpu.VMEM((HEAD, length), F32),
            pltpu.VMEM((HEAD, length), F32),
        ],
        cost_estimate=pl.CostEstimate(
            flops=10 * heads * HEAD * tokens * length,
            transcendentals=heads * tokens * length,
            bytes_accessed=heads * HEAD * (8 * tokens + 12 * length),
        ),
        name="attend_back",
    )(query[0], keys[0], values[0], *extra, logs, grad)
    return (
        dq.reshape(heads * HEAD, tokens),
        dkv.reshape(2 * heads * HEAD, length),
        jnp.sum(gain_q[:, :, 0], 0),
        jnp.sum(gain_k[:, :, 0], 0),
    )


def norm(members, width):
    first = sum(jnp.sum(m, 0) for m in members)
    second = sum(jnp.sum(m * m, 0) for m in members)
    sums = total(jnp.stack([first, second]))
    average = sums[0] / width
    scale = lax.rsqrt(sums[1] / width - average * average + EPS)
    return tuple((m - average) * scale for m in members), scale


def norm_back(grads, normals, scale, width):
    first = sum(jnp.sum(g, 0) for g in grads)
    second = sum(jnp.sum(g * n, 0) for g, n in zip(grads, normals))
    sums = total(jnp.stack([first, second])) / width
    return tuple((g - sums[0] - n * sums[1]) * scale for g, n in zip(grads, normals))


def tables(positions):
    quarter = HEAD // 4
    frequency = BASE ** (-(jnp.arange(quarter, dtype=F32) / quarter))
    place = positions.astype(F32)
    angles = jnp.concatenate([frequency[:, None] * place[0], frequency[:, None] * place[1]], 0)
    return jnp.cos(angles), jnp.sin(angles)


def gelu(u):
    return jax.nn.gelu(u, approximate=True)


def shards(
    latents,
    skip_latents,
    text_states,
    condition,
    positions,
    cotangent,
    w_skip,
    g_skip,
    g_norm1,
    w_mod,
    w_qkv,
    g_query,
    g_key,
    w_out,
    g_norm3,
    w_cross_q,
    w_cross_kv,
    g_cross_q,
    g_cross_k,
    w_cross_out,
    g_norm2,
    w_fc1,
    w_fc2,
):
    me = lax.axis_index("col")
    count = latents.shape[0]
    each = range(count)
    part = latents.shape[2]
    width = 4 * part
    members = lax.axis_size("dp") * lax.axis_size("row")
    wide = lax.axis_index(WIDE)
    direct = members == 8
    mine = jnp.stack([me ^ m for m in ORDER]).astype(jnp.int32)
    keep = jnp.zeros((1,), jnp.int32)

    def gather(shard):
        full = lax.all_gather(shard, WIDE, axis=0, tiled=True)
        return take_blocks(full.reshape((4, full.shape[0] // 4) + full.shape[1:]), mine)

    def fetch(shard):
        if not direct:
            return jnp.concatenate([gather(s) for s in shard], 0)
        blocks = wide_gather(shard)
        n = shard.shape[0]
        order = [
            ((2 * mine[j] + k) ^ wide) * n + s for s in range(n) for j in range(4) for k in range(2)
        ]
        return take_blocks(blocks, jnp.stack(order).astype(jnp.int32))

    def reduce(lefts, rights):
        grad = weight_grad(lefts, rights, mine, keep)
        return lax.psum_scatter(grad, WIDE, scatter_dimension=0, tiled=True).astype(F32)

    def send(lefts, rights):
        if not direct:
            return reduce(lefts, rights)
        turned = (wide & 1).astype(jnp.int32)[None]
        return wide_scatter(weight_grad(lefts, rights, mine ^ (wide >> 1), turned), BF16)

    full_skip = fetch(w_skip)
    full_qkv = fetch(jnp.concatenate([w_qkv[0], w_qkv[1], w_qkv[2]], 1)[None])
    full_out = fetch(w_out.T[None])
    full_cross_q = fetch(w_cross_q[None])
    full_cross_kv = fetch(jnp.concatenate([w_cross_kv[0], w_cross_kv[1]], 1)[None])
    full_cross_out = fetch(w_cross_out.T[None])
    full_fc1 = gather(w_fc1)
    full_fc2 = gather(w_fc2.T)

    cond_low = jax.nn.silu(condition.astype(F32)).astype(BF16)
    cond_mine = lax.dynamic_slice_in_dim(
        wide_gather(cond_low), wide * w_mod.shape[0], w_mod.shape[0], axis=1
    )
    shift = wide_scatter(dot("sd,de->se", cond_mine, w_mod), F32)

    col = lambda gain: gain[:, None]
    join = lambda *pieces: jnp.concatenate(sum(pieces, []), 0)
    low = lambda values: values.astype(BF16)
    image = [latents[i].T.astype(F32) for i in each]
    skip = [skip_latents[i].T.astype(F32) for i in each]
    text_length = text_states.shape[1]
    padded = -(-text_length // 128) * 128
    text_full = [
        join(spread(jnp.pad(text_states[i].T, ((0, 0), (0, padded - text_length))))) for i in each
    ]
    cot = [cotangent[i].T for i in each]
    turn = [tables(positions[i]) for i in each]
    in_heads = lambda values: values.reshape(-1, HEAD, values.shape[1])
    heads = part // HEAD

    normal_in, scale_in = zip(*[norm((image[i], skip[i]), 2 * width) for i in each])
    both_full = [
        join(
            spread(low(normal_in[i][0] * col(g_skip[0]))),
            spread(low(normal_in[i][1] * col(g_skip[1]))),
        )
        for i in each
    ]
    stream0 = [dot("de,dt->et", full_skip, both_full[i]) for i in each]
    normal_one, scale_one = zip(*[norm((stream0[i],), width) for i in each])
    ada_full = [
        join(spread(low(normal_one[i][0] * col(g_norm1) + col(shift[i])))) for i in each
    ]
    raw = [in_heads(dot("de,dt->et", full_qkv, ada_full[i])) for i in each]
    own = [
        ((raw[i], 0), (raw[i], heads), (raw[i], 2 * heads), (g_query, g_key), turn[i], True, raw[i].shape[2])
        for i in each
    ]
    attended, logs = zip(*[attend(*own[i]) for i in each])
    stream1 = [stream0[i] + settle(dot("ec,ct->et", full_out, attended[i])) for i in each]
    normal_three, scale_three = zip(*[norm((stream1[i],), width) for i in each])
    cross_full = [join(spread(low(normal_three[i][0] * col(g_norm3)))) for i in each]
    cross_raw = [in_heads(dot("de,dt->et", full_cross_q, cross_full[i])) for i in each]
    pair_raw = [in_heads(dot("de,dt->et", full_cross_kv, text_full[i])) for i in each]
    other = [
        ((cross_raw[i], 0), (pair_raw[i], 0), (pair_raw[i], heads), (g_cross_q, g_cross_k), turn[i], False, text_length)
        for i in each
    ]
    crossed, cross_logs = zip(*[attend(*other[i]) for i in each])
    stream2 = [stream1[i] + settle(dot("ec,ct->et", full_cross_out, crossed[i])) for i in each]
    normal_two, scale_two = zip(*[norm((stream2[i],), width) for i in each])
    mlp_full = [join(spread(low(normal_two[i][0] * col(g_norm2)))) for i in each]
    pre = [dot("de,dt->et", full_fc1, mlp_full[i]) for i in each]
    hidden, pulls = zip(*[jax.vjp(gelu, pre[i]) for i in each])
    hidden = [low(h) for h in hidden]
    output = [low(stream2[i] + settle(dot("ec,ct->et", full_fc2, hidden[i]))) for i in each]

    cot_full = [join(spread(cot[i])) for i in each]
    grad_pre = [low(pulls[i](dot("ec,et->ct", full_fc2, cot_full[i]))[0]) for i in each]
    grad_fc2 = reduce(cot_full, hidden).T
    grad_fc1 = reduce(mlp_full, grad_pre)
    grad_mlp = [settle(dot("de,et->dt", full_fc1, grad_pre[i])) for i in each]
    gain_two = sum(jnp.sum(grad_mlp[i] * normal_two[i][0], 1) for i in each)
    grad_stream2 = [
        cot[i].astype(F32)
        + norm_back((grad_mlp[i] * col(g_norm2),), normal_two[i], scale_two[i], width)[0]
        for i in each
    ]
    gs2_full = [join(spread(low(grad_stream2[i]))) for i in each]
    grad_crossed = [low(dot("ec,et->ct", full_cross_out, gs2_full[i])) for i in each]
    grad_cross_out = send(gs2_full, crossed).T
    grad_cq, grad_pair, gain_cq, gain_ck = zip(
        *[attend_back(*other[i], cross_logs[i], grad_crossed[i]) for i in each]
    )
    grad_cross_q = send(cross_full, grad_cq)
    grad_cross_kv = send(text_full, grad_pair)
    grad_cross_in = [settle(dot("de,et->dt", full_cross_q, grad_cq[i])) for i in each]
    grad_text = [
        settle(dot("de,et->dt", full_cross_kv, grad_pair[i]))[:, :text_length] for i in each
    ]
    gain_three = sum(jnp.sum(grad_cross_in[i] * normal_three[i][0], 1) for i in each)
    grad_stream1 = [
        grad_stream2[i]
        + norm_back((grad_cross_in[i] * col(g_norm3),), normal_three[i], scale_three[i], width)[0]
        for i in each
    ]
    gs1_full = [join(spread(low(grad_stream1[i]))) for i in each]
    grad_attended = [low(dot("ec,et->ct", full_out, gs1_full[i])) for i in each]
    grad_out = send(gs1_full, attended).T
    grad_q, grad_kv, gain_q, gain_k = zip(
        *[attend_back(*own[i], logs[i], grad_attended[i]) for i in each]
    )
    grad_qkv = [jnp.concatenate([grad_q[i], grad_kv[i]], 0) for i in each]
    grad_qkv_w = send(ada_full, grad_qkv)
    grad_ada = [settle(dot("de,et->dt", full_qkv, grad_qkv[i])) for i in each]
    grad_shift = jnp.stack([jnp.sum(grad_ada[i], 1) for i in each])
    grad_mod = jnp.einsum(
        "sd,se->de",
        cond_mine.astype(F32),
        wide_gather(grad_shift),
        precision=lax.Precision.HIGHEST,
    )
    gain_one = sum(jnp.sum(grad_ada[i] * normal_one[i][0], 1) for i in each)
    grad_stream0 = [
        low(
            grad_stream1[i]
            + norm_back((grad_ada[i] * col(g_norm1),), normal_one[i], scale_one[i], width)[0]
        )
        for i in each
    ]
    grad_skip_w = [
        send([both_full[i][s * width : (s + 1) * width] for i in each], grad_stream0)
        for s in range(2)
    ]
    back_both = [
        [
            settle(dot("de,et->dt", full_skip[s * width : (s + 1) * width], grad_stream0[i]))
            for s in range(2)
        ]
        for i in each
    ]
    gain_image, gain_skip = [
        sum(jnp.sum(back_both[i][s] * normal_in[i][s], 1) for i in each) for s in range(2)
    ]
    grad_in = [
        norm_back(
            [back_both[i][s] * col(g_skip[s]) for s in range(2)],
            normal_in[i],
            scale_in[i],
            2 * width,
        )
        for i in each
    ]
    head_sums = total(
        wide_sum(jnp.stack([sum(gain_q), sum(gain_k), sum(gain_cq), sum(gain_ck)]))
    )
    gain_sums = wide_sum(jnp.stack([gain_one, gain_three, gain_two]))
    skip_sums = wide_sum(jnp.stack([gain_image, gain_skip]))
    unstack = lambda grad, n: jnp.stack(jnp.split(grad, n, 1))
    back = lambda rows: jnp.stack([r.T for r in rows])
    return (
        back(output),
        back([g[0] for g in grad_in]),
        back([g[1] for g in grad_in]),
        back(grad_text),
        jnp.stack(grad_skip_w),
        skip_sums,
        gain_sums[0],
        grad_mod,
        unstack(grad_qkv_w, 3),
        head_sums[0],
        head_sums[1],
        grad_out,
        gain_sums[1],
        grad_cross_q,
        unstack(grad_cross_kv, 2),
        head_sums[2],
        head_sums[3],
        grad_cross_out,
        gain_sums[2],
        grad_fc1,
        grad_fc2,
    )


def solution(mesh):
    wide = ("dp", "row")
    tokens, rows, stacked, columns = (
        P(wide, None, "col"),
        P(wide, "col"),
        P(None, wide, "col"),
        P("col", wide),
    )
    gain = P("col")
    return jax.shard_map(
        shards,
        mesh=mesh,
        in_specs=(
            tokens,
            tokens,
            tokens,
            P(wide, None),
            P(wide, None, None),
            tokens,
            stacked,
            P(None, "col"),
            gain,
            rows,
            stacked,
            P(),
            P(),
            columns,
            gain,
            rows,
            stacked,
            P(),
            P(),
            columns,
            gain,
            rows,
            columns,
        ),
        out_specs=(
            tokens,
            tokens,
            tokens,
            tokens,
            stacked,
            P(None, "col"),
            gain,
            rows,
            stacked,
            P(),
            P(),
            columns,
            gain,
            rows,
            stacked,
            P(),
            P(),
            columns,
            gain,
            rows,
            columns,
        ),
        check_vma=False,
    )
```
